32 devices in a mesh: src: 4 (over z), dst: 8 (over y, x, core).
Axes of the slice: x: 2, y: 2, z: 4, core: 2. Of those that a mesh axis runs over, the one named last changes fastest.
Arguments:
- src_emb: bfloat16 [65536, 128], P('src'), may hold values from -1.5 to 1.5
- dst_emb: bfloat16 [65536, 128], P('dst'), may hold values from -1.5 to 1.5
- out_emb: bfloat16 [65536, 128], P('dst'), may hold values from -1.5 to 1.5
- word_table: bfloat16 [32768, 128], P('dst'), may hold values from -1.5 to 1.5
- log_norm: float32 [65536], P('dst'), may hold values from 9 to 11
- block_mask: int32 [128, 128], P('src', 'dst'), may hold values from 0 to 1, as said below
- tokens: int32 [3, 8], replicated, may hold values from 0 to 32767
- alpha_start: float32 [8, 65536], P(None, 'src'), may hold values from 0.5 to 80
- beta_end: float32 [8, 65536], P(None, 'dst'), may hold values from 0.5 to 80
Outputs:
- alpha_end: float32 [8, 65536], P(None, 'dst')
- beta_start: float32 [8, 65536], P(None, 'src')
- block_counts: float32 [128, 128], P('src', 'dst')
The draws below stay inside these ranges and needn't reach their ends.
Inputs may be any that keep to these rules, and one draw needn't show every extreme that they name: block_mask[I, I] = 1 for every block I: a state may always move within its own block.
All inputs are finite; a program needn't handle non-finite values.
Results may differ from the reference program's by a relative error of at most 0.0032.
Values may be sent and summed in bfloat16 or wider, within the bound.
A program may use at most 384 MiB of HBM per device.

```python
import math
import jax
import jax.numpy as jnp
import numpy as np
from jax import lax

S = 65536
BLK = 512
E = 128
V = 32768
TRACES = 8
STEPS = 3
NB = 128


def draw_src_emb(key, part):
    values = jnp.clip(0.3 * jax.random.normal(jax.random.fold_in(key, 1), (S, E), jnp.float32), -1.5, 1.5)
    return values.astype(jnp.bfloat16)


def draw_dst_emb(key, part):
    values = jnp.clip(0.3 * jax.random.normal(jax.random.fold_in(key, 2), (S, E), jnp.float32), -1.5, 1.5)
    return values.astype(jnp.bfloat16)


def rising_vector(key, salt):
    position = jnp.arange(S, dtype=jnp.float32) / S
    ramp = jnp.exp(jnp.log(10.0) * position)
    rough = jnp.exp(jax.random.uniform(jax.random.fold_in(key, salt), (TRACES, S), jnp.float32, -0.69, 0.69))
    return ramp[None, :] * rough


def draw_alpha_start(key, part):
    return rising_vector(key, 11)


def draw_beta_end(key, part):
    return rising_vector(key, 13)


def draw_block_mask(key, part):
    coin_flips = jax.random.randint(key, (NB, NB), 0, 16)
    rows = jnp.arange(NB)[:, None]
    cols = jnp.arange(NB)[None, :]
    diagonal = rows == cols
    near = jnp.abs(rows - cols) <= NB // 8
    keep = diagonal | near & (coin_flips < 8) | (coin_flips == 0)
    return jnp.where(keep, 1, 0).astype(jnp.int32)


def place_ends(drawn, key, low, largest):
    longest = drawn.shape.index(max(drawn.shape))
    spots = []
    for shift in (0, 1):
        where = [jax.random.randint(jax.random.fold_in(key, axis), (), 0, length) for axis, length in enumerate(drawn.shape)]
        where[longest] = (where[longest] + shift) % drawn.shape[longest]
        spots.append(tuple(where))
    return drawn.at[spots[0]].set(low).at[spots[1]].set(largest)


def block_scale(key, dims, split, low, largest):
    level, own = 1.0, jax.random.fold_in(key, 6)
    for dim, shards_of in split:
        steps = jnp.exp(jax.random.uniform(jax.random.fold_in(own, dim), (shards_of,), jnp.float32, low / len(split), largest / len(split)))
        level = level * jnp.repeat(steps, dims[dim] // shards_of).reshape([-1 if axis == dim else 1 for axis in range(len(dims))])
    return level


def rank_bounds(number_of, slope):
    portions = [(1 << 20) // math.isqrt(grade ** slope) + 1 for grade in range(1, number_of + 1)]
    scale = 1 + sum(portions) // (1 << 30)
    return np.cumsum(np.array([max(1, weight // scale) for weight in portions]))


def ranked(rng, extent, number_of, skew):
    listing = rank_bounds(number_of, skew)
    pick = jax.random.randint(jax.random.fold_in(rng, 1), extent, 0, int(listing[number_of - 1]))
    grade = jnp.searchsorted(jnp.asarray(listing, jnp.int32), pick, side="right")
    return jax.random.permutation(jax.random.fold_in(rng, 2), number_of)[grade].astype(jnp.int32)


def gaussian(key, shape, deviation, most, shards=(), kind=jnp.bfloat16):
    values = deviation * jax.random.normal(key, shape, jnp.float32)
    if shards:
        values = values * block_scale(key, shape, shards, -0.22, 0.18)
    return jnp.clip(values, -most, most).astype(kind)


def setup_inputs(seed: int = 0) -> dict:
    key_of = jax.random.split(jax.random.key(seed), 10)
    src_emb = draw_src_emb(jax.random.fold_in(key_of[9], 71), 0)
    dst_emb = draw_dst_emb(jax.random.fold_in(key_of[9], 71), 0)
    out_emb = gaussian(key_of[2], (S, E), 0.3, 1.5, ((0, 8),))
    word_table = gaussian(key_of[3], (V, E), 0.3, 1.5, ((0, 8),))
    log_norm = jnp.clip(9.0 + 2.0 * jax.random.uniform(key_of[4], (S,), jnp.float32) ** block_scale(key_of[4], (S,), ((0, 8),), -0.2, 0.2), 9.0, 11.0)
    block_mask = draw_block_mask(jax.random.fold_in(key_of[9], 71), 0)
    tokens = place_ends(ranked(key_of[6], (STEPS, TRACES), V, 2), jax.random.fold_in(key_of[6], 3), 0, V - 1).astype(jnp.int32)
    alpha_start = draw_alpha_start(jax.random.fold_in(key_of[9], 71), 0)
    beta_end = draw_beta_end(jax.random.fold_in(key_of[9], 71), 0)
    return dict(src_emb=src_emb, dst_emb=dst_emb, out_emb=out_emb, word_table=word_table, log_norm=log_norm, block_mask=block_mask, tokens=tokens, alpha_start=alpha_start, beta_end=beta_end)


very_negative = -1e30


def block_tables(src_rows, dst_emb, mask_row):
    scores = jnp.dot(src_rows, dst_emb.T, preferred_element_type=jnp.float32)
    scores = scores.reshape(src_rows.shape[0], NB, BLK)
    block_top = jnp.max(scores, axis=2)
    block_sum = jnp.sum(jnp.exp(scores - block_top[:, :, None]), axis=2)
    allowed = (mask_row == 1)[None, :]
    row_best = jnp.max(jnp.where(allowed, block_top, very_negative), axis=1)
    row_mass = jnp.sum(jnp.where(allowed, block_sum * jnp.exp(block_top - row_best[:, None]), 0.0), axis=1)
    log_total = row_best + jnp.log(row_mass)
    factor = jnp.where(allowed, jnp.exp(block_top - log_total[:, None]), 0.0)
    transit = jnp.where(allowed[:, :, None], jnp.exp(scores - block_top[:, :, None]), 0.0).astype(jnp.bfloat16)
    return factor, transit


def sweep(src_emb, dst_emb, block_mask, alphas, weights):
    members = alphas.shape[0]
    traces = alphas.shape[1]
    src_blocks = src_emb.reshape(NB, BLK, E)
    alpha_blocks = alphas.reshape(members, traces, NB, BLK).transpose(2, 0, 1, 3)
    weight_cols = weights.reshape(members, traces, NB, BLK).astype(jnp.float32)

    def one_block(running, inputs):
        src_rows, mask_row, alpha_rows = inputs
        factor, transit = block_tables(src_rows, dst_emb, mask_row)
        transit_wide = transit.astype(jnp.float32)
        mix_terms = (alpha_rows[:, :, :, None] * factor[None, None]).astype(jnp.bfloat16)
        mix_wide = mix_terms.astype(jnp.float32)
        running = running + jnp.einsum("abin,inc->abnc", mix_wide, transit_wide)
        spread = jnp.einsum("inc,abnc->abin", transit_wide, weight_cols)
        partial_value = jnp.sum(factor[None, None] * spread, axis=3)
        block_terms = jnp.sum(mix_wide * spread, axis=2)
        return running, (partial_value, block_terms)

    zeros_start = jnp.zeros((members, traces, NB, BLK), jnp.float32)
    predicted, (partial_value, block_terms) = lax.scan(one_block, zeros_start, (src_blocks, block_mask, alpha_blocks))
    predicted = predicted.reshape(members, traces, S)
    partial_value = partial_value.transpose(1, 2, 0, 3).reshape(members, traces, S)
    return predicted, partial_value, block_terms


def normalize(vector):
    return vector / (jnp.sum(vector, axis=1, keepdims=True) / S)


def reference(src_emb, dst_emb, out_emb, word_table, log_norm, block_mask, tokens, alpha_start, beta_end):
    traces = tokens.shape[1]
    word_rows = word_table[tokens.reshape(-1)]
    logits = jnp.dot(word_rows, out_emb.T, preferred_element_type=jnp.float32)
    emission = jnp.exp(logits - log_norm[None, :]).reshape(STEPS, traces, S)
    alphas = [alpha_start]
    beta_store = {STEPS: beta_end}

    def weight_at(k):
        return (emission[k - 1] * beta_store[k]).astype(jnp.bfloat16)

    for k in range(1, STEPS):
        predicted, partial_value, _ = sweep(src_emb, dst_emb, block_mask, alphas[k - 1][None], weight_at(STEPS - k + 1)[None])
        alphas.append(normalize(predicted[0] * emission[k - 1]))
        beta_store[STEPS - k] = normalize(partial_value[0])
    final_alphas = jnp.stack(alphas)
    final_weights = jnp.stack([weight_at(t + 1) for t in range(STEPS)])
    predicted, partial_value, block_terms = sweep(src_emb, dst_emb, block_mask, final_alphas, final_weights)
    alpha_end = normalize(predicted[STEPS - 1] * emission[STEPS - 1])
    beta_start = normalize(partial_value[0])
    pair_total = jnp.sum(block_terms, axis=(0, 3))
    counts = jnp.sum(block_terms / pair_total[None, :, :, None], axis=(1, 2)) * (NB * NB / (STEPS * traces))
    return alpha_end, beta_start, counts
```

```python
import functools

import jax
import jax.numpy as jnp
from jax import lax
from jax.experimental import pallas as pl
from jax.experimental.pallas import tpu as pltpu
from jax.sharding import PartitionSpec as P

BLK = 512
STEPS = 3
NB = 128
LANES = 128
DEPTH = 8
very_negative = -1e30
VMEM_BYTES = 60 * 1024 * 1024


def table_kernel(unit, cols, ids, count, src, dst, top, mass, transit, buf, sems):
    number = count[0]
    chunk = min(256, unit)

    def copy(slot, b):
        return pltpu.make_async_copy(buf.at[b], transit.at[slot], sems.at[b])

    def body(slot, carry):
        b = lax.rem(slot, 2)
        entry = ids[slot]
        i = lax.div(entry, cols)
        j = lax.rem(entry, cols)

        @pl.when(slot >= 2)
        def _():
            copy(slot - 2, b).wait()

        d = dst[pl.ds(pl.multiple_of(j * BLK, BLK), BLK), :]
        for c in range(unit // chunk):
            base = pl.multiple_of(i * unit + c * chunk, chunk)
            scores = lax.dot_general(
                d, src[pl.ds(base, chunk), :], (((1,), (1,)), ((), ())),
                preferred_element_type=jnp.float32,
            )
            best = jnp.max(scores, axis=0, keepdims=True)
            risen = jnp.exp(scores - best)
            buf[b, :, c * chunk:(c + 1) * chunk] = risen.astype(jnp.bfloat16)
            top[pl.ds(j, 1), pl.ds(base, chunk)] = best
            mass[pl.ds(j, 1), pl.ds(base, chunk)] = jnp.sum(risen, axis=0, keepdims=True)
        copy(slot, b).start()
        return carry

    lax.fori_loop(0, number, body, 0)
    for back in (2, 1):

        @pl.when(number >= back)
        def _():
            copy(number - back, lax.rem(number - back, 2)).wait()


def sweep_kernel(unit, cols, traces, kind, ids, count, *refs):
    if kind == 2:
        alpha, early, factor, weight, transit, pred, carried, terms, buf, sems = refs
    elif kind == 1:
        alpha, factor, weight, transit, pred, carried, terms, buf, sems = refs
    else:
        alpha, factor, weight, transit, pred, carried, buf, sems = refs
    number = count[0]
    pred[...] = jnp.zeros_like(pred)
    carried[...] = jnp.zeros_like(carried)
    if kind:
        terms[...] = jnp.zeros_like(terms)

    def copy(slot, b):
        return pltpu.make_async_copy(transit.at[slot], buf.at[b], sems.at[b])

    for p in range(DEPTH):

        @pl.when(p < number)
        def _():
            copy(p, p).start()

    def body(slot, carry):
        b = lax.rem(slot, DEPTH)
        entry = ids[slot]
        i = lax.div(entry, cols)
        j = lax.rem(entry, cols)
        rows = pl.ds(pl.multiple_of(i * unit, unit), unit)
        places = pl.ds(pl.multiple_of(j * BLK, BLK), BLK)
        share = factor[pl.ds(j, 1), rows]
        mix = (alpha[:, rows] * share).astype(jnp.bfloat16)
        w = weight[:, places].astype(jnp.bfloat16)
        copy(slot, b).wait()
        pred[:, places] += lax.dot_general(
            mix, buf[b], (((1,), (1,)), ((), ())), preferred_element_type=jnp.float32
        )
        spread = jnp.dot(w, buf[b], preferred_element_type=jnp.float32)
        carried[:, rows] += share * spread[:traces]

        @pl.when(slot + DEPTH < number)
        def _():
            copy(slot + DEPTH, b).start()

        if kind:
            group = pl.ds(pl.multiple_of(lax.div(entry, LANES) * LANES, LANES), LANES)
            hit = lax.broadcasted_iota(jnp.int32, (traces, LANES), 1) == lax.rem(entry, LANES)

            def note(t, m, s):
                value = jnp.sum(m.astype(jnp.float32) * s, axis=1, keepdims=True)
                terms[t, :, group] += jnp.where(hit, value, 0.0)

            if kind == 1:
                note(0, mix, spread)
            else:
                first = (early[:, rows] * share).astype(jnp.bfloat16)
                note(0, first, spread[:traces])
                note(1, mix, spread[traces:])
        return carry

    lax.fori_loop(0, number, body, 0)


def local(
    src_emb, dst_emb, out_emb, word_table, log_norm, block_mask, tokens, alpha_start, beta_end
):
    row_count, emb_width = src_emb.shape
    col_count = dst_emb.shape[0]
    traces = alpha_start.shape[0]
    src_count = lax.axis_size("src")
    dst_count = lax.axis_size("dst")
    states = row_count * src_count
    group = dst_count // src_count
    piece = col_count // src_count
    unit = min(BLK, piece)
    units = row_count // unit
    cols = col_count // BLK
    places = units * cols
    padded = -(-places // LANES) * LANES
    src_place = lax.axis_index("src")
    dst_place = lax.axis_index("dst")
    both = ("src", "dst")
    moves = [
        ((d // group) * dst_count + (d % group) * src_count + z, z * dst_count + d)
        for z in range(src_count)
        for d in range(dst_count)
    ]

    def spread_rows(mine):
        moved = lax.ppermute(mine, both, moves)
        return lax.all_gather(moved, "dst", axis=0, tiled=True)

    mine = lax.dynamic_slice_in_dim(src_emb, dst_place * piece, piece, 0)
    src_rows = spread_rows(mine)
    alpha_piece = lax.dynamic_slice_in_dim(alpha_start, dst_place * piece, piece, 1)
    alpha_moved = lax.ppermute(alpha_piece, both, moves)
    alpha_rows = lax.all_gather(alpha_moved, "dst", axis=1, tiled=True)

    whole_mask = lax.all_gather(block_mask, "src", axis=0, tiled=True)
    unit_index = jnp.arange(units, dtype=jnp.int32)
    per_piece = piece // unit
    unit_state = (
        (unit_index // per_piece) * col_count + src_place * piece + (unit_index % per_piece) * unit
    )
    unit_block = unit_state // BLK
    owner = unit_block[:, None] == jnp.arange(whole_mask.shape[0], dtype=jnp.int32)[None, :]
    mask = jnp.sum(jnp.where(owner[:, :, None], whole_mask[None], 0), axis=1)
    flat = (mask == 1).reshape(places)
    index = jnp.arange(places, dtype=jnp.int32)
    before = jnp.sum(
        jnp.where((index[None, :] < index[:, None]) & flat[None, :], 1, 0), axis=1
    )
    ids = jnp.sum(
        jnp.where((before[None, :] == index[:, None]) & flat[None, :], index[None, :], 0), axis=1
    ).astype(jnp.int32)
    number = jnp.sum(flat.astype(jnp.int32)).reshape(1)

    smem = pl.BlockSpec(memory_space=pltpu.SMEM)
    vmem = pl.BlockSpec(memory_space=pltpu.VMEM)
    anywhere = pl.BlockSpec(memory_space=pl.ANY)
    guess = places // 5 + 1
    params = pltpu.CompilerParams(vmem_limit_bytes=VMEM_BYTES)
    top, mass, transit = pl.pallas_call(
        functools.partial(table_kernel, unit, cols),
        out_shape=(
            jax.ShapeDtypeStruct((cols, row_count), jnp.float32),
            jax.ShapeDtypeStruct((cols, row_count), jnp.float32),
            jax.ShapeDtypeStruct((places, BLK, unit), jnp.bfloat16),
        ),
        in_specs=[smem, smem, vmem, vmem],
        out_specs=(vmem, vmem, anywhere),
        scratch_shapes=[
            pltpu.VMEM((2, BLK, unit), jnp.bfloat16),
            pltpu.SemaphoreType.DMA((2,)),
        ],
        compiler_params=params,
        cost_estimate=pl.CostEstimate(
            flops=guess * BLK * unit * emb_width * 2,
            bytes_accessed=guess * BLK * unit * 2,
            transcendentals=guess * BLK * unit,
        ),
        name="table",
    )(ids, number, src_rows, dst_emb)

    vocab_slice = word_table.shape[0]
    local_ids = tokens.reshape(-1) - dst_place * vocab_slice
    onehot = (local_ids[:, None] == jnp.arange(vocab_slice, dtype=jnp.int32)[None, :]).astype(
        jnp.bfloat16
    )
    looked = jnp.dot(onehot, word_table, preferred_element_type=jnp.float32)
    word_rows = lax.psum(looked.astype(jnp.bfloat16), "dst")
    logits = lax.dot_general(
        word_rows, out_emb, (((1,), (1,)), ((), ())), preferred_element_type=jnp.float32
    )
    emission = jnp.exp(logits - log_norm[None, :]).reshape(STEPS, traces, col_count)
    emission_piece = lax.dynamic_slice_in_dim(emission, src_place * piece, piece, 2)

    allowed = jnp.repeat((mask == 1).T, unit, axis=1)
    row_best = jnp.max(jnp.where(allowed, top, very_negative), axis=0)
    row_mass = jnp.sum(jnp.where(allowed, mass * jnp.exp(top - row_best[None, :]), 0.0), axis=0)
    pairs = lax.all_gather(jnp.stack([row_best, row_mass]), "dst", axis=0)
    whole_best = jnp.max(pairs[:, 0], axis=0)
    whole_mass = jnp.sum(pairs[:, 1] * jnp.exp(pairs[:, 0] - whole_best[None]), axis=0)
    log_total = whole_best + jnp.log(whole_mass)
    factor = jnp.where(allowed, jnp.exp(top - log_total[None, :]), 0.0)

    def sweep(kind, alphas, weights):
        outs = [
            jax.ShapeDtypeStruct((traces, col_count), jnp.float32),
            jax.ShapeDtypeStruct((traces, row_count), jnp.float32),
        ]
        if kind:
            outs.append(jax.ShapeDtypeStruct((kind, traces, padded), jnp.float32))
        return pl.pallas_call(
            functools.partial(sweep_kernel, unit, cols, traces, kind),
            out_shape=tuple(outs),
            in_specs=[smem, smem] + [vmem] * (len(alphas) + 2) + [anywhere],
            out_specs=(vmem,) * len(outs),
            scratch_shapes=[
                pltpu.VMEM((DEPTH, BLK, unit), jnp.bfloat16),
                pltpu.SemaphoreType.DMA((DEPTH,)),
            ],
            compiler_params=params,
            cost_estimate=pl.CostEstimate(
                flops=guess * BLK * unit * traces * 4,
                bytes_accessed=guess * BLK * unit * 2,
                transcendentals=0,
            ),
            name="sweep%d" % kind,
        )(ids, number, *alphas, factor, weights, transit)

    def tail(value):
        return jnp.broadcast_to(value[:, None, None], (traces, 1, LANES))

    def exchange_forward(partial_value, position):
        scale = jnp.sum(partial_value * emission[position], axis=1)
        payload = jnp.concatenate(
            [
                partial_value.reshape(traces, src_count, piece),
                jnp.broadcast_to(tail(scale), (traces, src_count, LANES)),
            ],
            axis=2,
        )
        part = lax.psum_scatter(payload, "src", scatter_dimension=1, tiled=False)
        part = jnp.concatenate(
            [part[:, :piece] * emission_piece[position], part[:, piece:]], axis=1
        )
        gathered = lax.all_gather(part, "dst", axis=1)
        total = jnp.sum(gathered[:, :, piece], axis=1) / states
        return gathered[:, :, :piece].reshape(traces, row_count) / total[:, None]

    def exchange_backward(partial_value):
        scale = jnp.sum(partial_value, axis=1)
        payload = jnp.concatenate(
            [
                partial_value.reshape(traces, dst_count, piece),
                jnp.broadcast_to(tail(scale), (traces, dst_count, LANES)),
            ],
            axis=2,
        )
        part = lax.psum_scatter(payload, "dst", scatter_dimension=1, tiled=False)
        gathered = lax.all_gather(part, "src", axis=1)
        total = jnp.sum(gathered[:, :, piece], axis=1) / states
        return gathered[:, :, :piece].reshape(traces, col_count) / total[:, None]

    last_weights = emission[2] * beta_end
    pred, carried = sweep(0, [alpha_rows], last_weights)
    alpha_1 = exchange_forward(pred, 0)
    weights_2 = emission[1] * exchange_backward(carried)
    pred, carried, middle_terms = sweep(1, [alpha_1], weights_2)
    alpha_2 = exchange_forward(pred, 1)
    weights_1 = emission[0] * exchange_backward(carried)
    pred, carried, end_terms = sweep(
        2, [alpha_2, alpha_rows], jnp.concatenate([weights_1, last_weights], axis=0)
    )

    block_terms = jnp.concatenate([middle_terms, end_terms], axis=0)[:, :, :places]
    scales = jnp.concatenate(
        [
            jnp.sum(pred * emission[2], axis=1)[None],
            jnp.sum(carried, axis=1)[None],
            jnp.sum(block_terms, axis=2),
        ],
        axis=0,
    )
    totals = lax.psum(scales, both)
    predicted = lax.psum(pred, "src")
    alpha_end = predicted * emission[2] / (totals[0] / states)[:, None]

    part = lax.psum_scatter(
        carried.reshape(traces, dst_count, piece), "dst", scatter_dimension=1, tiled=False
    )
    back = lax.ppermute(part, both, [(b, a) for a, b in moves])
    gathered = lax.all_gather(back, "dst", axis=1, tiled=True)
    beta_start = gathered / (totals[1] / states)[:, None]

    counts = jnp.sum(block_terms / totals[2:][:, :, None], axis=(0, 1)) * (
        NB * NB / (STEPS * traces)
    )
    counts = counts.reshape(units, cols)
    placed = jnp.sum(jnp.where(owner[:, :, None], counts[:, None, :], 0.0), axis=0)
    block_counts = lax.psum_scatter(placed, "src", scatter_dimension=0, tiled=True)
    return (alpha_end, beta_start, block_counts)


def solution(mesh):
    return jax.shard_map(
        local,
        mesh=mesh,
        in_specs=(
            P("src", None),
            P("dst", None),
            P("dst", None),
            P("dst", None),
            P("dst"),
            P("src", "dst"),
            P(),
            P(None, "src"),
            P(None, "dst"),
        ),
        out_specs=(P(None, "dst"), P(None, "src"), P("src", "dst")),
        check_vma=False,
    )
```

```python
import functools

import jax
import jax.numpy as jnp
from jax import lax
from jax.experimental import pallas as pl
from jax.experimental.pallas import tpu as pltpu
from jax.sharding import PartitionSpec as P

BLK = 512
STEPS = 3
NB = 128
LANES = 128
DEPTH = 8
very_negative = -1e30
VMEM_BYTES = 60 * 1024 * 1024


def table_kernel(unit, cols, ids, count, src, dst, top, mass, transit, buf, sems):
    number = count[0]
    chunk = min(256, unit)

    def copy(slot, b):
        return pltpu.make_async_copy(buf.at[b], transit.at[slot], sems.at[b])

    def body(slot, carry):
        b = lax.rem(slot, 2)
        entry = ids[slot]
        i = lax.div(entry, cols)
        j = lax.rem(entry, cols)

        @pl.when(slot >= 2)
        def _():
            copy(slot - 2, b).wait()

        d = dst[pl.ds(pl.multiple_of(j * BLK, BLK), BLK), :]
        for c in range(unit // chunk):
            base = pl.multiple_of(i * unit + c * chunk, chunk)
            scores = lax.dot_general(
                d, src[pl.ds(base, chunk), :], (((1,), (1,)), ((), ())),
                preferred_element_type=jnp.float32,
            )
            best = jnp.max(scores, axis=0, keepdims=True)
            risen = jnp.exp(scores - best)
            buf[b, :, c * chunk:(c + 1) * chunk] = risen.astype(jnp.bfloat16)
            top[pl.ds(j, 1), pl.ds(base, chunk)] = best
            mass[pl.ds(j, 1), pl.ds(base, chunk)] = jnp.sum(risen, axis=0, keepdims=True)
        copy(slot, b).start()
        return carry

    lax.fori_loop(0, number, body, 0)
    for back in (2, 1):

        @pl.when(number >= back)
        def _():
            copy(number - back, lax.rem(number - back, 2)).wait()


def sweep_kernel(unit, cols, traces, kind, ids, count, *refs):
    if kind == 2:
        alpha, early, factor, weight, transit, pred, carried, terms, buf, sems = refs
    elif kind == 1:
        alpha, factor, weight, transit, pred, carried, terms, buf, sems = refs
    else:
        alpha, factor, weight, transit, pred, carried, buf, sems = refs
    number = count[0]
    pred[...] = jnp.zeros_like(pred)
    carried[...] = jnp.zeros_like(carried)
    if kind:
        terms[...] = jnp.zeros_like(terms)

    def copy(slot, b):
        return pltpu.make_async_copy(transit.at[slot], buf.at[b], sems.at[b])

    for p in range(DEPTH):

        @pl.when(p < number)
        def _():
            copy(p, p).start()

    def body(slot, carry):
        b = lax.rem(slot, DEPTH)
        entry = ids[slot]
        i = lax.div(entry, cols)
        j = lax.rem(entry, cols)
        rows = pl.ds(pl.multiple_of(i * unit, unit), unit)
        places = pl.ds(pl.multiple_of(j * BLK, BLK), BLK)
        share = factor[pl.ds(j, 1), rows]
        mix = (alpha[:, rows] * share).astype(jnp.bfloat16)
        w = weight[:, places].astype(jnp.bfloat16)
        copy(slot, b).wait()
        pred[:, places] += lax.dot_general(
            mix, buf[b], (((1,), (1,)), ((), ())), preferred_element_type=jnp.float32
        )
        spread = jnp.dot(w, buf[b], preferred_element_type=jnp.float32)
        carried[:, rows] += share * spread[:traces]

        @pl.when(slot + DEPTH < number)
        def _():
            copy(slot + DEPTH, b).start()

        if kind:
            group = pl.ds(pl.multiple_of(lax.div(entry, LANES) * LANES, LANES), LANES)
            hit = lax.broadcasted_iota(jnp.int32, (traces, LANES), 1) == lax.rem(entry, LANES)

            def note(t, m, s):
                value = jnp.sum(m.astype(jnp.float32) * s, axis=1, keepdims=True)
                terms[t, :, group] += jnp.where(hit, value, 0.0)

            if kind == 1:
                note(0, mix, spread)
            else:
                first = (early[:, rows] * share).astype(jnp.bfloat16)
                note(0, first, spread[:traces])
                note(1, mix, spread[traces:])
        return carry

    lax.fori_loop(0, number, body, 0)


def exchange_kernel(
    lines, piece, states, ahead, behind, glow, alpha, beta,
    in_f, in_b, red_f, red_b, land_f, land_b, send_1, recv_1, send_2, recv_2,
):
    place = {name: lax.axis_index(name) for name in lines}
    mesh_ids = pl.DeviceIdType.MESH

    def peer(name, k):
        return lax.rem(place[name] + k, lines[name])

    def origin(name, k):
        return lax.rem(place[name] + lines[name] - k, lines[name])

    barrier = pltpu.get_barrier_semaphore()
    for name in lines:
        for k in range(1, lines[name]):
            pl.semaphore_signal(
                barrier, inc=1, device_id={name: peer(name, k)}, device_id_type=mesh_ids
            )
    pl.semaphore_wait(barrier, sum(lines.values()) - len(lines))

    offset = {"src": 0, "dst": lines["src"]}
    payload = {"src": ahead, "dst": behind}
    landing = {"src": in_f, "dst": in_b}
    first = {"src": [], "dst": []}
    for name in lines:
        for k in range(1, lines[name]):
            copy = pltpu.make_async_remote_copy(
                src_ref=payload[name].at[peer(name, k)],
                dst_ref=landing[name].at[k],
                send_sem=send_1.at[offset[name] + k],
                recv_sem=recv_1.at[offset[name] + k],
                device_id={name: peer(name, k)},
                device_id_type=mesh_ids,
            )
            copy.start()
            first[name].append(copy)
    second = []
    for name, other, red, land in (("src", "dst", red_f, land_f), ("dst", "src", red_b, land_b)):
        value = payload[name][place[name]]
        for k in range(1, lines[name]):
            first[name][k - 1].wait_recv()
            value = value + landing[name][k]
        if name == "src":
            value = jnp.concatenate([value[:, :piece] * glow[...], value[:, piece:]], axis=1)
        red[...] = value
        for k in range(1, lines[other]):
            copy = pltpu.make_async_remote_copy(
                src_ref=red,
                dst_ref=land.at[k],
                send_sem=send_2.at[offset[other] + k],
                recv_sem=recv_2.at[offset[other] + k],
                device_id={other: peer(other, k)},
                device_id_type=mesh_ids,
            )
            copy.start()
            second.append(copy)
    for copy in second:
        copy.wait_recv()
    for other, red, land, out in (("dst", red_f, land_f, alpha), ("src", red_b, land_b, beta)):
        total = red[:, piece:piece + 1]
        for k in range(1, lines[other]):
            total = total + land[k, :, piece:piece + 1]
        scale = total / states
        for k in range(lines[other]):
            part = red[:, :piece] if k == 0 else land[k, :, :piece]
            start = pl.multiple_of(origin(other, k) * piece, piece)
            out[:, pl.ds(start, piece)] = part / scale
    for copies in (first["src"], first["dst"], second):
        for copy in copies:
            copy.wait_send()


def local(
    src_emb, dst_emb, out_emb, word_table, log_norm, block_mask, tokens, alpha_start, beta_end
):
    row_count, emb_width = src_emb.shape
    col_count = dst_emb.shape[0]
    traces = alpha_start.shape[0]
    src_count = lax.axis_size("src")
    dst_count = lax.axis_size("dst")
    states = row_count * src_count
    group = dst_count // src_count
    piece = col_count // src_count
    unit = min(BLK, piece)
    units = row_count // unit
    cols = col_count // BLK
    places = units * cols
    padded = -(-places // LANES) * LANES
    src_place = lax.axis_index("src")
    dst_place = lax.axis_index("dst")
    both = ("src", "dst")
    moves = [
        ((d // group) * dst_count + (d % group) * src_count + z, z * dst_count + d)
        for z in range(src_count)
        for d in range(dst_count)
    ]

    def spread_rows(mine):
        moved = lax.ppermute(mine, both, moves)
        return lax.all_gather(moved, "dst", axis=0, tiled=True)

    mine = lax.dynamic_slice_in_dim(src_emb, dst_place * piece, piece, 0)
    src_rows = spread_rows(mine)
    alpha_piece = lax.dynamic_slice_in_dim(alpha_start, dst_place * piece, piece, 1)
    alpha_moved = lax.ppermute(alpha_piece, both, moves)
    alpha_rows = lax.all_gather(alpha_moved, "dst", axis=1, tiled=True)

    whole_mask = lax.all_gather(block_mask, "src", axis=0, tiled=True)
    unit_index = jnp.arange(units, dtype=jnp.int32)
    per_piece = piece // unit
    unit_state = (
        (unit_index // per_piece) * col_count + src_place * piece + (unit_index % per_piece) * unit
    )
    unit_block = unit_state // BLK
    owner = unit_block[:, None] == jnp.arange(whole_mask.shape[0], dtype=jnp.int32)[None, :]
    mask = jnp.sum(jnp.where(owner[:, :, None], whole_mask[None], 0), axis=1)
    flat = (mask == 1).reshape(places)
    index = jnp.arange(places, dtype=jnp.int32)
    before = jnp.sum(
        jnp.where((index[None, :] < index[:, None]) & flat[None, :], 1, 0), axis=1
    )
    ids = jnp.sum(
        jnp.where((before[None, :] == index[:, None]) & flat[None, :], index[None, :], 0), axis=1
    ).astype(jnp.int32)
    number = jnp.sum(flat.astype(jnp.int32)).reshape(1)

    smem = pl.BlockSpec(memory_space=pltpu.SMEM)
    vmem = pl.BlockSpec(memory_space=pltpu.VMEM)
    anywhere = pl.BlockSpec(memory_space=pl.ANY)
    guess = places // 5 + 1
    params = pltpu.CompilerParams(vmem_limit_bytes=VMEM_BYTES)
    top, mass, transit = pl.pallas_call(
        functools.partial(table_kernel, unit, cols),
        out_shape=(
            jax.ShapeDtypeStruct((cols, row_count), jnp.float32),
            jax.ShapeDtypeStruct((cols, row_count), jnp.float32),
            jax.ShapeDtypeStruct((places, BLK, unit), jnp.bfloat16),
        ),
        in_specs=[smem, smem, vmem, vmem],
        out_specs=(vmem, vmem, anywhere),
        scratch_shapes=[
            pltpu.VMEM((2, BLK, unit), jnp.bfloat16),
            pltpu.SemaphoreType.DMA((2,)),
        ],
        compiler_params=params,
        cost_estimate=pl.CostEstimate(
            flops=guess * BLK * unit * emb_width * 2,
            bytes_accessed=guess * BLK * unit * 2,
            transcendentals=guess * BLK * unit,
        ),
        name="table",
    )(ids, number, src_rows, dst_emb)

    vocab_slice = word_table.shape[0]
    local_ids = tokens.reshape(-1) - dst_place * vocab_slice
    onehot = (local_ids[:, None] == jnp.arange(vocab_slice, dtype=jnp.int32)[None, :]).astype(
        jnp.bfloat16
    )
    looked = jnp.dot(onehot, word_table, preferred_element_type=jnp.float32)
    word_rows = lax.psum(looked.astype(jnp.bfloat16), "dst")
    logits = lax.dot_general(
        word_rows, out_emb, (((1,), (1,)), ((), ())), preferred_element_type=jnp.float32
    )
    emission = jnp.exp(logits - log_norm[None, :]).reshape(STEPS, traces, col_count)
    emission_piece = lax.dynamic_slice_in_dim(emission, src_place * piece, piece, 2)

    allowed = jnp.repeat((mask == 1).T, unit, axis=1)
    row_best = jnp.max(jnp.where(allowed, top, very_negative), axis=0)
    row_mass = jnp.sum(jnp.where(allowed, mass * jnp.exp(top - row_best[None, :]), 0.0), axis=0)
    pairs = lax.all_gather(jnp.stack([row_best, row_mass]), "dst", axis=0)
    whole_best = jnp.max(pairs[:, 0], axis=0)
    whole_mass = jnp.sum(pairs[:, 1] * jnp.exp(pairs[:, 0] - whole_best[None]), axis=0)
    log_total = whole_best + jnp.log(whole_mass)
    factor = jnp.where(allowed, jnp.exp(top - log_total[None, :]), 0.0)

    def sweep(kind, alphas, weights):
        outs = [
            jax.ShapeDtypeStruct((traces, col_count), jnp.float32),
            jax.ShapeDtypeStruct((traces, row_count), jnp.float32),
        ]
        if kind:
            outs.append(jax.ShapeDtypeStruct((kind, traces, padded), jnp.float32))
        return pl.pallas_call(
            functools.partial(sweep_kernel, unit, cols, traces, kind),
            out_shape=tuple(outs),
            in_specs=[smem, smem] + [vmem] * (len(alphas) + 2) + [anywhere],
            out_specs=(vmem,) * len(outs),
            scratch_shapes=[
                pltpu.VMEM((DEPTH, BLK, unit), jnp.bfloat16),
                pltpu.SemaphoreType.DMA((DEPTH,)),
            ],
            compiler_params=params,
            cost_estimate=pl.CostEstimate(
                flops=guess * BLK * unit * traces * 4,
                bytes_accessed=guess * BLK * unit * 2,
                transcendentals=0,
            ),
            name="sweep%d" % kind,
        )(ids, number, *alphas, factor, weights, transit)

    def exchange(ahead, behind, position):
        def payload(value, scale, number):
            return jnp.concatenate(
                [
                    value.reshape(traces, number, piece).transpose(1, 0, 2),
                    jnp.broadcast_to(scale[None, :, None], (number, traces, LANES)),
                ],
                axis=2,
            )

        width = piece + LANES
        semaphores = pltpu.SemaphoreType.DMA((src_count + dst_count,))
        return pl.pallas_call(
            functools.partial(
                exchange_kernel, {"src": src_count, "dst": dst_count}, piece, states
            ),
            out_shape=(
                jax.ShapeDtypeStruct((traces, row_count), jnp.float32),
                jax.ShapeDtypeStruct((traces, col_count), jnp.float32),
            ),
            in_specs=[vmem] * 3,
            out_specs=(vmem, vmem),
            scratch_shapes=[
                pltpu.VMEM((src_count, traces, width), jnp.float32),
                pltpu.VMEM((dst_count, traces, width), jnp.float32),
                pltpu.VMEM((traces, width), jnp.float32),
                pltpu.VMEM((traces, width), jnp.float32),
                pltpu.VMEM((dst_count, traces, width), jnp.float32),
                pltpu.VMEM((src_count, traces, width), jnp.float32),
            ]
            + [semaphores] * 4,
            compiler_params=pltpu.CompilerParams(
                collective_id=0, has_side_effects=True, vmem_limit_bytes=VMEM_BYTES
            ),
            name="exchange",
        )(
            payload(ahead, jnp.sum(ahead * emission[position], axis=1), src_count),
            payload(behind, jnp.sum(behind, axis=1), dst_count),
            emission_piece[position],
        )

    last_weights = emission[2] * beta_end
    pred, carried = sweep(0, [alpha_rows], last_weights)
    alpha_1, beta_2 = exchange(pred, carried, 0)
    weights_2 = emission[1] * beta_2
    pred, carried, middle_terms = sweep(1, [alpha_1], weights_2)
    alpha_2, beta_1 = exchange(pred, carried, 1)
    weights_1 = emission[0] * beta_1
    pred, carried, end_terms = sweep(
        2, [alpha_2, alpha_rows], jnp.concatenate([weights_1, last_weights], axis=0)
    )

    block_terms = jnp.concatenate([middle_terms, end_terms], axis=0)[:, :, :places]
    scales = jnp.concatenate(
        [
            jnp.sum(pred * emission[2], axis=1)[None],
            jnp.sum(carried, axis=1)[None],
            jnp.sum(block_terms, axis=2),
        ],
        axis=0,
    )
    totals = jnp.sum(lax.all_gather(scales, both, axis=0), axis=0)
    predicted = jnp.sum(lax.all_gather(pred, "src", axis=0), axis=0)
    alpha_end = predicted * emission[2] / (totals[0] / states)[:, None]

    parts = carried.reshape(traces, dst_count, piece).transpose(1, 0, 2)
    part = jnp.sum(lax.all_to_all(parts, "dst", 0, 0, tiled=False), axis=0)
    back = lax.ppermute(part, both, [(b, a) for a, b in moves])
    gathered = lax.all_gather(back, "dst", axis=1, tiled=True)
    beta_start = gathered / (totals[1] / states)[:, None]

    counts = jnp.sum(block_terms / totals[2:][:, :, None], axis=(0, 1)) * (
        NB * NB / (STEPS * traces)
    )
    counts = counts.reshape(units, cols)
    placed = jnp.sum(jnp.where(owner[:, :, None], counts[:, None, :], 0.0), axis=0)
    mask_rows = block_mask.shape[0]
    everyone = jnp.sum(lax.all_gather(placed, "src", axis=0), axis=0)
    block_counts = lax.dynamic_slice_in_dim(everyone, src_place * mask_rows, mask_rows, 0)
    return (alpha_end, beta_start, block_counts)


def solution(mesh):
    return jax.shard_map(
        local,
        mesh=mesh,
        in_specs=(
            P("src", None),
            P("dst", None),
            P("dst", None),
            P("dst", None),
            P("dst"),
            P("src", "dst"),
            P(),
            P(None, "src"),
            P(None, "dst"),
        ),
        out_specs=(P(None, "dst"), P(None, "src"), P("src", "dst")),
        check_vma=False,
    )
```

```python
import functools

import jax
import jax.numpy as jnp
from jax import lax
from jax.experimental import pallas as pl
from jax.experimental.pallas import tpu as pltpu
from jax.sharding import PartitionSpec as P

BLK = 512
STEPS = 3
NB = 128
LANES = 128
DEPTH = 8
very_negative = -1e30
VMEM_BYTES = 60 * 1024 * 1024


def table_kernel(unit, cols, ids, count, src, dst, top, mass, transit, buf, sems):
    number = count[0]
    chunk = min(256, unit)

    def copy(slot, b):
        return pltpu.make_async_copy(buf.at[b], transit.at[slot], sems.at[b])

    def body(slot, carry):
        b = lax.rem(slot, 2)
        entry = ids[slot]
        i = lax.div(entry, cols)
        j = lax.rem(entry, cols)

        @pl.when(slot >= 2)
        def _():
            copy(slot - 2, b).wait()

        d = dst[pl.ds(pl.multiple_of(j * BLK, BLK), BLK), :]
        for c in range(unit // chunk):
            base = pl.multiple_of(i * unit + c * chunk, chunk)
            scores = lax.dot_general(
                d, src[pl.ds(base, chunk), :], (((1,), (1,)), ((), ())),
                preferred_element_type=jnp.float32,
            )
            best = jnp.max(scores, axis=0, keepdims=True)
            risen = jnp.exp(scores - best)
            buf[b, :, c * chunk:(c + 1) * chunk] = risen.astype(jnp.bfloat16)
            top[pl.ds(j, 1), pl.ds(base, chunk)] = best
            mass[pl.ds(j, 1), pl.ds(base, chunk)] = jnp.sum(risen, axis=0, keepdims=True)
        copy(slot, b).start()
        return carry

    lax.fori_loop(0, number, body, 0)
    for back in (2, 1):

        @pl.when(number >= back)
        def _():
            copy(number - back, lax.rem(number - back, 2)).wait()


def sweep_kernel(unit, cols, traces, kind, ids, count, *refs):
    if kind == 2:
        alpha, early, factor, weight, transit, pred, carried, terms, buf, sems = refs
    elif kind == 1:
        alpha, factor, weight, transit, pred, carried, terms, buf, sems = refs
    else:
        alpha, factor, weight, transit, pred, carried, buf, sems = refs
    number = count[0]
    pred[...] = jnp.zeros_like(pred)
    carried[...] = jnp.zeros_like(carried)
    if kind:
        terms[...] = jnp.zeros_like(terms)

    def copy(slot, b):
        return pltpu.make_async_copy(transit.at[slot], buf.at[b], sems.at[b])

    for p in range(DEPTH):

        @pl.when(p < number)
        def _():
            copy(p, p).start()

    def body(slot, carry):
        b = lax.rem(slot, DEPTH)
        entry = ids[slot]
        i = lax.div(entry, cols)
        j = lax.rem(entry, cols)
        rows = pl.ds(pl.multiple_of(i * unit, unit), unit)
        places = pl.ds(pl.multiple_of(j * BLK, BLK), BLK)
        share = factor[pl.ds(j, 1), rows]
        mix = (alpha[:, rows] * share).astype(jnp.bfloat16)
        w = weight[:, places].astype(jnp.bfloat16)
        copy(slot, b).wait()
        pred[:, places] += lax.dot_general(
            mix, buf[b], (((1,), (1,)), ((), ())), preferred_element_type=jnp.float32
        )
        spread = jnp.dot(w, buf[b], preferred_element_type=jnp.float32)
        carried[:, rows] += share * spread[:traces]

        @pl.when(slot + DEPTH < number)
        def _():
            copy(slot + DEPTH, b).start()

        if kind:
            group = pl.ds(pl.multiple_of(lax.div(entry, LANES) * LANES, LANES), LANES)
            hit = lax.broadcasted_iota(jnp.int32, (traces, LANES), 1) == lax.rem(entry, LANES)

            def note(t, m, s):
                value = jnp.sum(m.astype(jnp.float32) * s, axis=1, keepdims=True)
                terms[t, :, group] += jnp.where(hit, value, 0.0)

            if kind == 1:
                note(0, mix, spread)
            else:
                first = (early[:, rows] * share).astype(jnp.bfloat16)
                note(0, first, spread[:traces])
                note(1, mix, spread[traces:])
        return carry

    lax.fori_loop(0, number, body, 0)


def exchange_kernel(
    lines, piece, states, ahead, behind, glow, alpha, beta,
    in_f, in_b, red_f, red_b, land_f, land_b, send_1, recv_1, send_2, recv_2,
):
    place = {name: lax.axis_index(name) for name in lines}
    mesh_ids = pl.DeviceIdType.MESH

    def peer(name, k):
        return lax.rem(place[name] + k, lines[name])

    def origin(name, k):
        return lax.rem(place[name] + lines[name] - k, lines[name])

    barrier = pltpu.get_barrier_semaphore()
    for name in lines:
        for k in range(1, lines[name]):
            pl.semaphore_signal(
                barrier, inc=1, device_id={name: peer(name, k)}, device_id_type=mesh_ids
            )
    pl.semaphore_wait(barrier, sum(lines.values()) - len(lines))

    offset = {"src": 0, "dst": lines["src"]}
    payload = {"src": ahead, "dst": behind}
    landing = {"src": in_f, "dst": in_b}
    first = {"src": [], "dst": []}
    for name in lines:
        for k in range(1, lines[name]):
            copy = pltpu.make_async_remote_copy(
                src_ref=payload[name].at[peer(name, k)],
                dst_ref=landing[name].at[k],
                send_sem=send_1.at[offset[name] + k],
                recv_sem=recv_1.at[offset[name] + k],
                device_id={name: peer(name, k)},
                device_id_type=mesh_ids,
            )
            copy.start()
            first[name].append(copy)
    second = []
    for name, other, red, land in (("src", "dst", red_f, land_f), ("dst", "src", red_b, land_b)):
        value = payload[name][place[name]]
        for k in range(1, lines[name]):
            first[name][k - 1].wait_recv()
            value = value + landing[name][k]
        if name == "src":
            value = jnp.concatenate([value[:, :piece] * glow[...], value[:, piece:]], axis=1)
        red[...] = value
        for k in range(1, lines[other]):
            copy = pltpu.make_async_remote_copy(
                src_ref=red,
                dst_ref=land.at[k],
                send_sem=send_2.at[offset[other] + k],
                recv_sem=recv_2.at[offset[other] + k],
                device_id={other: peer(other, k)},
                device_id_type=mesh_ids,
            )
            copy.start()
            second.append(copy)
    for copy in second:
        copy.wait_recv()
    for other, red, land, out in (("dst", red_f, land_f, alpha), ("src", red_b, land_b, beta)):
        total = red[:, piece:piece + 1]
        for k in range(1, lines[other]):
            total = total + land[k, :, piece:piece + 1]
        scale = total / states
        for k in range(lines[other]):
            part = red[:, :piece] if k == 0 else land[k, :, :piece]
            start = pl.multiple_of(origin(other, k) * piece, piece)
            out[:, pl.ds(start, piece)] = part / scale
    for copies in (first["src"], first["dst"], second):
        for copy in copies:
            copy.wait_send()


def total_kernel(lines, value, out, red, land_1, land_2, send_1, recv_1, send_2, recv_2):
    place = {name: lax.axis_index(name) for name in lines}
    mesh_ids = pl.DeviceIdType.MESH

    def peer(name, k):
        return lax.rem(place[name] + k, lines[name])

    barrier = pltpu.get_barrier_semaphore()
    for name in lines:
        for k in range(1, lines[name]):
            pl.semaphore_signal(
                barrier, inc=1, device_id={name: peer(name, k)}, device_id_type=mesh_ids
            )
    pl.semaphore_wait(barrier, sum(lines.values()) - len(lines))

    def line_sum(name, given, land, send, recv):
        copies = []
        for k in range(1, lines[name]):
            copy = pltpu.make_async_remote_copy(
                src_ref=given,
                dst_ref=land.at[k],
                send_sem=send.at[k],
                recv_sem=recv.at[k],
                device_id={name: peer(name, k)},
                device_id_type=mesh_ids,
            )
            copy.start()
            copies.append(copy)
        total = given[...]
        for k in range(1, lines[name]):
            copies[k - 1].wait_recv()
            total = total + land[k]
        return total, copies

    red[...], early = line_sum("src", value, land_1, send_1, recv_1)
    out[...], late = line_sum("dst", red, land_2, send_2, recv_2)
    for copy in early + late:
        copy.wait_send()


def local(
    src_emb, dst_emb, out_emb, word_table, log_norm, block_mask, tokens, alpha_start, beta_end
):
    row_count, emb_width = src_emb.shape
    col_count = dst_emb.shape[0]
    traces = alpha_start.shape[0]
    src_count = lax.axis_size("src")
    dst_count = lax.axis_size("dst")
    states = row_count * src_count
    group = dst_count // src_count
    piece = col_count // src_count
    unit = min(BLK, piece)
    units = row_count // unit
    cols = col_count // BLK
    places = units * cols
    padded = -(-places // LANES) * LANES
    src_place = lax.axis_index("src")
    dst_place = lax.axis_index("dst")
    both = ("src", "dst")
    moves = [
        ((d // group) * dst_count + (d % group) * src_count + z, z * dst_count + d)
        for z in range(src_count)
        for d in range(dst_count)
    ]

    def spread_rows(mine):
        moved = lax.ppermute(mine, both, moves)
        return lax.all_gather(moved, "dst", axis=0, tiled=True)

    mine = lax.dynamic_slice_in_dim(src_emb, dst_place * piece, piece, 0)
    src_rows = spread_rows(mine)
    alpha_piece = lax.dynamic_slice_in_dim(alpha_start, dst_place * piece, piece, 1)
    alpha_moved = lax.ppermute(alpha_piece, both, moves)
    alpha_rows = lax.all_gather(alpha_moved, "dst", axis=1, tiled=True)

    whole_mask = lax.all_gather(block_mask, "src", axis=0, tiled=True)
    unit_index = jnp.arange(units, dtype=jnp.int32)
    per_piece = piece // unit
    unit_state = (
        (unit_index // per_piece) * col_count + src_place * piece + (unit_index % per_piece) * unit
    )
    unit_block = unit_state // BLK
    owner = unit_block[:, None] == jnp.arange(whole_mask.shape[0], dtype=jnp.int32)[None, :]
    mask = jnp.sum(jnp.where(owner[:, :, None], whole_mask[None], 0), axis=1)
    flat = (mask == 1).reshape(places)
    index = jnp.arange(places, dtype=jnp.int32)
    before = jnp.sum(
        jnp.where((index[None, :] < index[:, None]) & flat[None, :], 1, 0), axis=1
    )
    ids = jnp.sum(
        jnp.where((before[None, :] == index[:, None]) & flat[None, :], index[None, :], 0), axis=1
    ).astype(jnp.int32)
    number = jnp.sum(flat.astype(jnp.int32)).reshape(1)

    smem = pl.BlockSpec(memory_space=pltpu.SMEM)
    vmem = pl.BlockSpec(memory_space=pltpu.VMEM)
    anywhere = pl.BlockSpec(memory_space=pl.ANY)
    guess = places // 5 + 1
    params = pltpu.CompilerParams(vmem_limit_bytes=VMEM_BYTES)
    top, mass, transit = pl.pallas_call(
        functools.partial(table_kernel, unit, cols),
        out_shape=(
            jax.ShapeDtypeStruct((cols, row_count), jnp.float32),
            jax.ShapeDtypeStruct((cols, row_count), jnp.float32),
            jax.ShapeDtypeStruct((places, BLK, unit), jnp.bfloat16),
        ),
        in_specs=[smem, smem, vmem, vmem],
        out_specs=(vmem, vmem, anywhere),
        scratch_shapes=[
            pltpu.VMEM((2, BLK, unit), jnp.bfloat16),
            pltpu.SemaphoreType.DMA((2,)),
        ],
        compiler_params=params,
        cost_estimate=pl.CostEstimate(
            flops=guess * BLK * unit * emb_width * 2,
            bytes_accessed=guess * BLK * unit * 2,
            transcendentals=guess * BLK * unit,
        ),
        name="table",
    )(ids, number, src_rows, dst_emb)

    vocab_slice = word_table.shape[0]
    local_ids = tokens.reshape(-1) - dst_place * vocab_slice
    onehot = (local_ids[:, None] == jnp.arange(vocab_slice, dtype=jnp.int32)[None, :]).astype(
        jnp.bfloat16
    )
    looked = jnp.dot(onehot, word_table, preferred_element_type=jnp.float32)
    word_rows = lax.psum(looked.astype(jnp.bfloat16), "dst")
    logits = lax.dot_general(
        word_rows, out_emb, (((1,), (1,)), ((), ())), preferred_element_type=jnp.float32
    )
    emission = jnp.exp(logits - log_norm[None, :]).reshape(STEPS, traces, col_count)
    emission_piece = lax.dynamic_slice_in_dim(emission, src_place * piece, piece, 2)

    allowed = jnp.repeat((mask == 1).T, unit, axis=1)
    row_best = jnp.max(jnp.where(allowed, top, very_negative), axis=0)
    row_mass = jnp.sum(jnp.where(allowed, mass * jnp.exp(top - row_best[None, :]), 0.0), axis=0)
    pairs = lax.all_gather(jnp.stack([row_best, row_mass]), "dst", axis=0)
    whole_best = jnp.max(pairs[:, 0], axis=0)
    whole_mass = jnp.sum(pairs[:, 1] * jnp.exp(pairs[:, 0] - whole_best[None]), axis=0)
    log_total = whole_best + jnp.log(whole_mass)
    factor = jnp.where(allowed, jnp.exp(top - log_total[None, :]), 0.0)

    def sweep(kind, alphas, weights):
        outs = [
            jax.ShapeDtypeStruct((traces, col_count), jnp.float32),
            jax.ShapeDtypeStruct((traces, row_count), jnp.float32),
        ]
        if kind:
            outs.append(jax.ShapeDtypeStruct((kind, traces, padded), jnp.float32))
        return pl.pallas_call(
            functools.partial(sweep_kernel, unit, cols, traces, kind),
            out_shape=tuple(outs),
            in_specs=[smem, smem] + [vmem] * (len(alphas) + 2) + [anywhere],
            out_specs=(vmem,) * len(outs),
            scratch_shapes=[
                pltpu.VMEM((DEPTH, BLK, unit), jnp.bfloat16),
                pltpu.SemaphoreType.DMA((DEPTH,)),
            ],
            compiler_params=params,
            cost_estimate=pl.CostEstimate(
                flops=guess * BLK * unit * traces * 4,
                bytes_accessed=guess * BLK * unit * 2,
                transcendentals=0,
            ),
            name="sweep%d" % kind,
        )(ids, number, *alphas, factor, weights, transit)

    def exchange(ahead, behind, position):
        def payload(value, scale, number):
            return jnp.concatenate(
                [
                    value.reshape(traces, number, piece).transpose(1, 0, 2),
                    jnp.broadcast_to(scale[None, :, None], (number, traces, LANES)),
                ],
                axis=2,
            )

        width = piece + LANES
        semaphores = pltpu.SemaphoreType.DMA((src_count + dst_count,))
        return pl.pallas_call(
            functools.partial(
                exchange_kernel, {"src": src_count, "dst": dst_count}, piece, states
            ),
            out_shape=(
                jax.ShapeDtypeStruct((traces, row_count), jnp.float32),
                jax.ShapeDtypeStruct((traces, col_count), jnp.float32),
            ),
            in_specs=[vmem] * 3,
            out_specs=(vmem, vmem),
            scratch_shapes=[
                pltpu.VMEM((src_count, traces, width), jnp.float32),
                pltpu.VMEM((dst_count, traces, width), jnp.float32),
                pltpu.VMEM((traces, width), jnp.float32),
                pltpu.VMEM((traces, width), jnp.float32),
                pltpu.VMEM((dst_count, traces, width), jnp.float32),
                pltpu.VMEM((src_count, traces, width), jnp.float32),
            ]
            + [semaphores] * 4,
            compiler_params=pltpu.CompilerParams(
                collective_id=0, has_side_effects=True, vmem_limit_bytes=VMEM_BYTES
            ),
            name="exchange",
        )(
            payload(ahead, jnp.sum(ahead * emission[position], axis=1), src_count),
            payload(behind, jnp.sum(behind, axis=1), dst_count),
            emission_piece[position],
        )

    last_weights = emission[2] * beta_end
    pred, carried = sweep(0, [alpha_rows], last_weights)
    alpha_1, beta_2 = exchange(pred, carried, 0)
    weights_2 = emission[1] * beta_2
    pred, carried, middle_terms = sweep(1, [alpha_1], weights_2)
    alpha_2, beta_1 = exchange(pred, carried, 1)
    weights_1 = emission[0] * beta_1
    pred, carried, end_terms = sweep(
        2, [alpha_2, alpha_rows], jnp.concatenate([weights_1, last_weights], axis=0)
    )

    block_terms = jnp.concatenate([middle_terms, end_terms], axis=0)[:, :, :places]
    scales = jnp.concatenate(
        [
            jnp.sum(pred * emission[2], axis=1)[None],
            jnp.sum(carried, axis=1)[None],
            jnp.sum(block_terms, axis=2),
        ],
        axis=0,
    )
    kinds = scales.shape[0]
    shape = (-(-kinds // 8) * 8, -(-traces // LANES) * LANES)
    totals = pl.pallas_call(
        functools.partial(total_kernel, {"src": src_count, "dst": dst_count}),
        out_shape=jax.ShapeDtypeStruct(shape, jnp.float32),
        in_specs=[vmem],
        out_specs=vmem,
        scratch_shapes=[
            pltpu.VMEM(shape, jnp.float32),
            pltpu.VMEM((src_count,) + shape, jnp.float32),
            pltpu.VMEM((dst_count,) + shape, jnp.float32),
        ]
        + [pltpu.SemaphoreType.DMA((src_count,))] * 2
        + [pltpu.SemaphoreType.DMA((dst_count,))] * 2,
        compiler_params=pltpu.CompilerParams(collective_id=1, has_side_effects=True),
        name="totals",
    )(jnp.pad(scales, ((0, shape[0] - kinds), (0, shape[1] - traces))))[:kinds, :traces]
    predicted = jnp.sum(lax.all_gather(pred, "src", axis=0), axis=0)
    alpha_end = predicted * emission[2] / (totals[0] / states)[:, None]

    parts = carried.reshape(traces, dst_count, piece).transpose(1, 0, 2)
    part = jnp.sum(lax.all_to_all(parts, "dst", 0, 0, tiled=False), axis=0)
    back = lax.ppermute(part, both, [(b, a) for a, b in moves])
    gathered = lax.all_gather(back, "dst", axis=1, tiled=True)
    beta_start = gathered / (totals[1] / states)[:, None]

    counts = jnp.sum(block_terms / totals[2:][:, :, None], axis=(0, 1)) * (
        NB * NB / (STEPS * traces)
    )
    counts = counts.reshape(units, cols)
    placed = jnp.sum(jnp.where(owner[:, :, None], counts[:, None, :], 0.0), axis=0)
    mask_rows = block_mask.shape[0]
    everyone = jnp.sum(lax.all_gather(placed, "src", axis=0), axis=0)
    block_counts = lax.dynamic_slice_in_dim(everyone, src_place * mask_rows, mask_rows, 0)
    return (alpha_end, beta_start, block_counts)


def solution(mesh):
    return jax.shard_map(
        local,
        mesh=mesh,
        in_specs=(
            P("src", None),
            P("dst", None),
            P("dst", None),
            P("dst", None),
            P("dst"),
            P("src", "dst"),
            P(),
            P(None, "src"),
            P(None, "dst"),
        ),
        out_specs=(P(None, "dst"), P(None, "src"), P("src", "dst")),
        check_vma=False,
    )
```
